256 devices in a mesh: gx: 32 (over z, y_hi, core), gy: 8 (over y_lo, x).
Axes of the slice: x: 4, y: 4 (y_hi: 2, y_lo: 2; y = y_hi * 2 + y_lo), z: 8, core: 2. Of those that a mesh axis runs over, the one named last changes fastest.
Arguments:
- velocity: float32 [256, 256, 256], P('gx', 'gy'), may hold values from 1.5 to 4.5
- density: float32 [256, 256, 256], P('gx', 'gy'), may hold values from 1.8 to 2.6
- adjoint_last: float32 [256, 256, 256], P('gx', 'gy'), may hold values from -6 to 6
- adjoint_now: float32 [256, 256, 256], P('gx', 'gy'), may hold values from -6 to 6
- forward_accel: bfloat16 [8, 256, 256, 256], P(None, 'gx', 'gy'), may hold values from -6 to 6
- residual_panels: bfloat16 [131072, 128], P(('gx', 'gy')), may hold values from -6 to 6
- owner_slab: int32 [131072, 1], P(('gx', 'gy')), may hold values from 0 to 31; in each aligned block of 512 rows (0 to 511, 512 to 1023, ...) at most 32 rows name the same one
- receiver_cell: int32 [131072], P(('gx', 'gy')), may hold values from 0 to 65535
- trace_offset: int32 [131072], P(('gx', 'gy')), may hold values from 0 to 31
Outputs:
- sensitivity: float32 [128, 128, 128], P('gx', 'gy')
- adjoint_final: float32 [256, 256, 256], P('gx', 'gy')
The draws below stay inside these ranges and needn't reach their ends.
Inputs may be any that keep to these rules, and one draw needn't show every extreme that they name: `owner_slab`: the rows of one device name one slab at most 32 times, a bound that some block reaches. `receiver_cell`: numbered (x * 32 + y) * 256 + z within the owner's block.
All inputs are finite; a program needn't handle non-finite values.
Results may differ from the reference program's by a relative error of at most 0.0003.
Values may be sent and summed in bfloat16 or wider, within the bound.
A program may use at most 64 MiB of HBM per device.

```python
import math
import jax
import jax.numpy as jnp
import numpy as np

CX = 8
CY = 32
NZ = 256
SENS_DEV = 512
PANEL = 128
STEPS = 8
CAP = 32
NX = 256
NY = 256
SENSORS = 131072
N_GX = 32
N_GY = 8


def plant(result, rng, low, high):
    dims = result.shape
    index_at = [jax.random.randint(jax.random.fold_in(rng, axis), (), 0, dims[axis]) for axis in range(len(dims))]
    result = result.at[tuple(index_at)].set(low)
    longest = dims.index(max(dims))
    index_at[longest] = (index_at[longest] + 1) % dims[longest]
    return result.at[tuple(index_at)].set(high)


def steps_of(own_key, shape, cuts, low, high):
    factor_of, own = 1.0, jax.random.fold_in(own_key, 6)
    for axis_at, parts in cuts:
        draws = jnp.exp(jax.random.uniform(jax.random.fold_in(own, axis_at), (parts,), jnp.float32, low / len(cuts), high / len(cuts)))
        factor_of = factor_of * jnp.repeat(draws, shape[axis_at] // parts).reshape([-1 if axis == axis_at else 1 for axis in range(len(shape))])
    return factor_of


def shared_out(own_key, own, number, rows, count, top, most, skew):
    ranking = jax.random.permutation(own_key, count)
    crowded, ordinary = shares(count, rows * top, most, skew, True), shares(count, rows * top, most, skew, False)
    places = jnp.arange(count)

    def named(sizes, turn):
        used = int((sizes > 0).sum())
        fixed = max(1, used // 4)
        shifted = fixed + (places - fixed + turn * (used - fixed)) % max(1, count - fixed)
        return jnp.zeros((count,), jnp.int32).at[ranking[jnp.where(places < fixed, places, shifted)]].set(jnp.asarray(sizes, jnp.int32))

    sizes = jnp.where(number % 4 == 0, named(crowded, number // 4), named(ordinary, number - number // 4 - 1))
    mixed = jax.random.permutation(jax.random.fold_in(own, 3), count)
    source_of, receiver = mixed[0:count // 2 * 2:2], mixed[1:count // 2 * 2:2]
    slack = jnp.minimum(sizes[source_of] - 1, most - sizes[receiver]) // 2
    slack = jnp.where((source_of == ranking[0]) | (receiver == ranking[0]) | (sizes[receiver] == 0), 0, jnp.maximum(slack, 0))
    shifted = jax.random.randint(jax.random.fold_in(own, 4), (count // 2,), 0, 1 << 20) % (slack + 1)
    sizes = sizes.at[source_of].add(-shifted).at[receiver].add(shifted)
    items = jnp.searchsorted(jnp.cumsum(sizes), jnp.arange(rows * top), side="right").astype(jnp.int32)
    table = items.reshape(top, rows).T
    table = table[jax.random.permutation(jax.random.fold_in(own, 1), rows)]
    turn = jax.random.randint(jax.random.fold_in(own, 2), (rows, 1), 0, top)
    return jnp.take_along_axis(table, (jnp.arange(top)[None, :] + turn) % top, axis=1)


def shares(number_of, total, reach, lean, full):
    weights = [(1 << 20) // math.isqrt(rank ** lean) + 1 for rank in range(1, number_of + 1)]
    largest = reach if full else min(reach, max(-(-total // number_of), total * weights[0] // sum(weights)))
    least = 1 if total - largest >= number_of - 1 else 0
    counts, surplus = [largest] + [least] * (number_of - 1), total - largest - least * (number_of - 1)
    while surplus > 0:
        candidates = [i for i in range(1, number_of) if counts[i] < largest] or [i for i in range(1, number_of) if counts[i] < reach]
        mass, remaining = sum([weights[i] for i in candidates]), surplus
        for i in candidates:
            more = min(reach - counts[i], max(1, remaining * weights[i] // mass), surplus)
            counts[i] = counts[i] + more
            surplus = surplus - more
    return np.array(counts)


def centred(stream_key, shape, width, limit, cuts=(), kind=jnp.bfloat16):
    values = width * jax.random.normal(stream_key, shape, jnp.float32)
    if cuts:
        values = values * steps_of(stream_key, shape, cuts, -0.22, 0.18)
    return jnp.clip(values, -limit, limit).astype(kind)


def setup_inputs(seed: int = 0) -> dict:
    key_list = jax.random.split(jax.random.key(seed), 10)
    velocity = jnp.clip(1.5 + 3.0 * jax.random.uniform(key_list[0], (NX, NY, NZ), jnp.float32) ** steps_of(key_list[0], (NX, NY, NZ), ((0, 32), (1, 8)), -0.2, 0.2), 1.5, 4.5)
    density = jnp.clip(1.8 + 0.79999995 * jax.random.uniform(key_list[1], (NX, NY, NZ), jnp.float32) ** steps_of(key_list[1], (NX, NY, NZ), ((0, 32), (1, 8)), -0.2, 0.2), 1.8, 2.6)
    adjoint_last = centred(key_list[2], (NX, NY, NZ), 1.0, 6.0, ((0, 32), (1, 8)), jnp.float32)
    adjoint_now = centred(key_list[3], (NX, NY, NZ), 1.0, 6.0, ((0, 32), (1, 8)), jnp.float32)
    forward_accel = centred(key_list[4], (STEPS, NX, NY, NZ), 1.0, 6.0, ((1, 32), (2, 8)))
    residual_panels = centred(key_list[5], (SENSORS, PANEL), 1.0, 6.0, ((0, 256),))
    owner_slab_keys = jax.random.split(jax.random.fold_in(key_list[6], 1), SENSORS // SENS_DEV)
    owner_slab_turns = jax.random.permutation(jax.random.fold_in(key_list[6], 3), SENSORS // SENS_DEV)
    owner_slab = jax.vmap(lambda own, number: shared_out(jax.random.fold_in(key_list[6], 2), own, number, SENS_DEV, N_GX, 1, CAP, 2))(owner_slab_keys, owner_slab_turns).reshape((SENSORS, 1))
    receiver_cell = plant(jax.random.randint(key_list[7], (SENSORS,), 0, CX * CY * NZ), jax.random.fold_in(key_list[7], 1), 0, (CX * CY * NZ) - 1).astype(jnp.int32)
    trace_offset = plant(jax.random.randint(key_list[8], (SENSORS,), 0, 2 * PANEL // STEPS), jax.random.fold_in(key_list[8], 1), 0, (2 * PANEL // STEPS) - 1).astype(jnp.int32)
    return dict(velocity=velocity, density=density, adjoint_last=adjoint_last, adjoint_now=adjoint_now, forward_accel=forward_accel, residual_panels=residual_panels, owner_slab=owner_slab, receiver_cell=receiver_cell, trace_offset=trace_offset)


def resample(panels, offsets, step_count):
    panel_len = panels.shape[1]
    half_width = panel_len // step_count
    values = panels.astype(jnp.float32)
    clock = (jnp.arange(panel_len, dtype=jnp.int32)[None, :] + offsets[:, None]).astype(jnp.float32)
    columns = []
    for moment in range(step_count):
        weights = jnp.maximum(0.0, 1.0 - jnp.abs(clock - half_width * (moment + 1)) / half_width) * 0.25
        columns.append(jnp.sum(values * weights, axis=1))
    return jnp.stack(columns, axis=1)


def face_list(padded):
    return [padded[2:, 1:-1, 1:-1], padded[:-2, 1:-1, 1:-1],
            padded[1:-1, 2:, 1:-1], padded[1:-1, :-2, 1:-1],
            padded[1:-1, 1:-1, 2:], padded[1:-1, 1:-1, :-2]]


def coarsen(kernel):
    size_a, size_b, size_c = kernel.shape
    blocks = kernel.reshape(size_a // 2, 2, size_b // 2, 2, size_c // 2, 2)
    return jnp.sum(blocks, axis=(1, 3, 5)) * 0.125


def reference(velocity, density, adjoint_last, adjoint_now, forward_accel, residual_panels, owner_slab, receiver_cell, trace_offset):
    sensor_rows = jnp.arange(residual_panels.shape[0], dtype=jnp.int32)
    column_index = (sensor_rows // SENS_DEV) % N_GY
    owners = owner_slab[:, 0]
    local_x = receiver_cell // (CY * NZ)
    local_y = (receiver_cell // NZ) % CY
    local_z = receiver_cell % NZ
    global_cell = ((owners * CX + local_x) * NY + column_index * CY + local_y) * NZ + local_z
    amplitudes = resample(residual_panels, trace_offset, STEPS)
    square = 0.11 * velocity
    stiffness = square * square * density
    rho_pad = jnp.pad(density, 1)
    couplings = [stiffness * (2.0 / (density + nearby)) for nearby in face_list(rho_pad)]
    wave_prev = adjoint_last
    wave = adjoint_now
    accumulated = jnp.zeros(wave.shape, jnp.float32)
    for moment in range(STEPS):
        nearby = face_list(jnp.pad(wave, 1))
        laplace = couplings[0] * (nearby[0] - wave)
        for index in range(1, 6):
            laplace = laplace + couplings[index] * (nearby[index] - wave)
        wave_next = (2.0 * wave - wave_prev) + laplace
        wave_next = wave_next.reshape(-1).at[global_cell].add(amplitudes[:, moment]).reshape(wave.shape)
        accumulated = accumulated + wave_next * forward_accel[moment].astype(jnp.float32)
        wave_prev, wave = wave, wave_next
    kernel = (-2.0 / velocity) * accumulated
    sensitivity = jnp.transpose(coarsen(kernel), (0, 2, 1))
    return sensitivity, wave
```

```python
import functools

import jax
import jax.numpy as jnp
from jax import lax
from jax.experimental import pallas as pl
from jax.experimental.pallas import tpu as pltpu
from jax.sharding import PartitionSpec as P

MESH = pl.DeviceIdType.MESH
F32, BF16, I32 = jnp.float32, jnp.bfloat16, jnp.int32


def dot_nt(a, b):
    return lax.dot_general(a, b, (((1,), (1,)), ((), ())), preferred_element_type=F32)


def iota(shape, dim):
    return lax.broadcasted_iota(I32, shape, dim)


def halves(value):
    high = value.astype(BF16)
    return high, (value - high.astype(F32)).astype(BF16)


def build_messages(res_ref, owner, cell, offset, msg_ref, table_ref):
    row, k = iota((256, 128), 0), iota((256, 128), 1)
    gap = jnp.abs(k + row // 8 - 16 * (row % 8 + 1))
    weights = jnp.maximum(16 - gap, 0).astype(F32).astype(BF16)
    table_ref[...] = dot_nt(weights, res_ref[...])
    amp = jnp.zeros((8, 512), F32)
    for shift in range(32):
        amp = amp + jnp.where(offset == shift, table_ref[8 * shift : 8 * shift + 8, :], 0.0)
    amp = amp * (1.0 / 64.0)
    member = (iota((32, 512), 0) == owner).astype(F32)
    earlier = (iota((512, 512), 0) < iota((512, 512), 1)).astype(F32).astype(BF16)
    counts = jnp.dot(member.astype(BF16), earlier, preferred_element_type=F32)
    rank = jnp.sum(member * counts, axis=0, keepdims=True)
    slot = owner * 32 + rank.astype(I32)
    high, low = halves(amp)
    which = iota((16, 512), 0)
    digits = jnp.where(which == 0, cell // 256, jnp.where(which == 1, cell % 256, 0))
    payload = jnp.concatenate(
        [high.astype(F32), low.astype(F32), digits.astype(F32)], axis=0
    ).astype(BF16)
    place = (iota((1024, 512), 0) == slot).astype(F32).astype(BF16)
    packed = dot_nt(payload, place)
    lane = iota((8, 128), 1)
    for o in range(32):
        block = slice(128 * (o // 4), 128 * (o // 4) + 128)
        amps = packed[0:8, block] + packed[8:16, block]
        cells = packed[16:24, block]
        back = 32 * (o % 4)
        if back:
            amps = pltpu.roll(amps, 128 - back, 1)
        ahead = (32 - back) % 128
        if ahead:
            cells = pltpu.roll(cells, ahead, 1)
        msg_ref[o] = jnp.where(lane < 32, amps, cells)


def collect(recv_ref, amp_ref, xy_ref, z_ref):
    lane = iota((8, 128), 1)
    xs, zs = [], []
    for g in range(8):
        amps = jnp.zeros((8, 128), F32)
        cells = jnp.zeros((8, 128), F32)
        for q in range(4):
            tile = recv_ref[4 * g + q]
            here = (lane // 32) == q
            moved = pltpu.roll(tile, 32 * q, 1) if q else tile
            amps = jnp.where(here, moved, amps)
            turn = (32 * q - 32) % 128
            moved = pltpu.roll(tile, turn, 1) if turn else tile
            cells = jnp.where(here, moved, cells)
        amp_ref[:, 128 * g : 128 * g + 128] = amps
        xs.append(cells[0:1, :])
        zs.append(cells[1:2, :])
    rows = iota((256, 1024), 0).astype(F32)
    xy_ref[...] = (rows == jnp.concatenate(xs, axis=1)).astype(F32).astype(BF16)
    z_ref[...] = (rows == jnp.concatenate(zs, axis=1)).astype(F32).astype(BF16)


def kernel(
    last_ref, now_ref, dens_ref, vel_ref, facc_hbm, res_ref, owner_ref, cell_ref, offset_ref,
    sens_ref, final_ref,
    wave, rho, ysend, yrecv, rsend, rrecv, coef, source, acc, facc, msg, recv, table,
    amp, xy, zz, usend, urecv,
    ss, rs, ds, dr, as_, ar, us, ur, fs,
):
    i, j = lax.axis_index("gx"), lax.axis_index("gy")
    nx, ny = 32, 8
    left, right = lax.rem(i + nx - 1, nx), lax.rem(i + 1, nx)
    lower, upper = lax.rem(j + ny - 1, ny), lax.rem(j + 1, ny)
    barrier = pltpu.get_barrier_semaphore()

    def greet_x(k, c):
        pl.semaphore_signal(
            barrier, inc=1, device_id=(lax.rem(i + k, nx), j), device_id_type=MESH
        )
        return c

    def greet_y(k, c):
        pl.semaphore_signal(
            barrier, inc=1, device_id=(i, lax.rem(j + k, ny)), device_id_type=MESH
        )
        return c

    lax.fori_loop(1, nx, greet_x, 0)
    lax.fori_loop(1, ny, greet_y, 0)
    forward = pltpu.make_async_copy(facc_hbm, facc, fs)
    forward.start()

    for x in range(8):
        ysend[0, 0, x : x + 1, :] = now_ref[x, 0:1, :]
        ysend[0, 1, x : x + 1, :] = now_ref[x, 31:32, :]
        rsend[0, x : x + 1, :] = dens_ref[x, 0:1, :]
        rsend[1, x : x + 1, :] = dens_ref[x, 31:32, :]
    wave[0, 1:9] = now_ref[...]
    wave[1, 1:9] = last_ref[...]
    rho[1:9] = dens_ref[...]
    build_messages(res_ref, owner_ref[...], cell_ref[...], offset_ref[...], msg, table)
    recv[i] = msg[i]
    acc[...] = jnp.zeros_like(acc)
    pl.semaphore_wait(barrier, nx + ny - 2)

    def remote(src, dst, send, receive, device):
        return pltpu.make_async_remote_copy(
            src_ref=src, dst_ref=dst, send_sem=send, recv_sem=receive,
            device_id=device, device_id_type=MESH,
        )

    def scatter(k):
        to = lax.rem(i + k, nx)
        return remote(msg.at[to], recv.at[i], as_.at[k], ar.at[k], (to, j))

    def begin(k, c):
        scatter(k).start()
        return c

    def end(k, c):
        scatter(k).wait()
        return c

    lax.fori_loop(1, nx, begin, 0)
    edges = [
        remote(dens_ref.at[0], rho.at[9], ds.at[0], dr.at[0], (left, j)),
        remote(dens_ref.at[7], rho.at[0], ds.at[1], dr.at[1], (right, j)),
        remote(rsend.at[0], rrecv.at[1], ds.at[2], dr.at[2], (i, lower)),
        remote(rsend.at[1], rrecv.at[0], ds.at[3], dr.at[3], (i, upper)),
        remote(now_ref.at[0], wave.at[0, 9], ss.at[0, 0], rs.at[0, 0], (left, j)),
        remote(now_ref.at[7], wave.at[0, 0], ss.at[0, 1], rs.at[0, 1], (right, j)),
    ]

    def halo_x(p):
        return [
            remote(wave.at[p, 1], wave.at[p, 9], ss.at[p, 0], rs.at[p, 0], (left, j)),
            remote(wave.at[p, 8], wave.at[p, 0], ss.at[p, 1], rs.at[p, 1], (right, j)),
        ]

    def halo_y(p):
        return [
            remote(ysend.at[p, 0], yrecv.at[p, 1], ss.at[p, 2], rs.at[p, 2], (i, lower)),
            remote(ysend.at[p, 1], yrecv.at[p, 0], ss.at[p, 3], rs.at[p, 3], (i, upper)),
        ]

    for copy in edges + halo_y(0):
        copy.start()
    for copy in edges[:4]:
        copy.wait()

    row, lane = iota((32, 256), 0), iota((32, 256), 1)
    has_low, has_high = (j > 0).astype(F32), (j < ny - 1).astype(F32)

    def couple(x, c):
        density = rho[x + 1]
        speed = 0.11 * vel_ref[x]
        stiff = speed * speed * density
        first = jnp.where(jnp.logical_and(x == 0, i == 0), 0.0, 1.0)
        final = jnp.where(jnp.logical_and(x == 7, i == nx - 1), 0.0, 1.0)
        low = rrecv[0, pl.ds(x, 1), :] * has_low
        high = rrecv[1, pl.ds(x, 1), :] * has_high
        near = [
            (rho[x + 2] * final, final),
            (rho[x] * first, first),
            (
                jnp.where(row == 31, high, pltpu.roll(density, 31, 0)),
                jnp.where(row == 31, has_high, 1.0),
            ),
            (
                jnp.where(row == 0, low, pltpu.roll(density, 1, 0)),
                jnp.where(row == 0, has_low, 1.0),
            ),
            (
                jnp.where(lane == 255, 0.0, pltpu.roll(density, 255, 1)),
                jnp.where(lane == 255, 0.0, 1.0),
            ),
            (
                jnp.where(lane == 0, 0.0, pltpu.roll(density, 1, 1)),
                jnp.where(lane == 0, 0.0, 1.0),
            ),
        ]
        centre = 2.0
        for n, (value, inside) in enumerate(near):
            strength = stiff * (2.0 / (density + value))
            centre = centre - strength
            coef[n + 1, x] = strength * inside
        coef[0, x] = centre
        return c

    lax.fori_loop(0, 8, couple, 0)
    lax.fori_loop(1, nx, end, 0)
    collect(recv, amp, xy, zz)

    def inject(t):
        high, low = halves(amp[pl.ds(t, 1), :])
        cells = xy[...]
        source[...] = (
            dot_nt(cells * high, zz[...]) + dot_nt(cells * low, zz[...])
        ).reshape(8, 32, 256)

    inject(0)
    forward.wait()

    def layer(t, p, x, out):
        w = wave[p, x + 1]
        up = jnp.where(row == 31, yrecv[p, 1, x : x + 1, :], pltpu.roll(w, 31, 0))
        down = jnp.where(row == 0, yrecv[p, 0, x : x + 1, :], pltpu.roll(w, 1, 0))
        value = coef[0, x] * w + (source[x] - wave[1 - p, x + 1])
        value = value + coef[1, x] * wave[p, x + 2] + coef[2, x] * wave[p, x]
        value = value + coef[3, x] * up + coef[4, x] * down
        value = value + coef[5, x] * pltpu.roll(w, 255, 1) + coef[6, x] * pltpu.roll(w, 1, 1)
        acc[x] += value * facc[t, x].astype(F32)
        if out:
            final_ref[x] = value
        else:
            wave[1 - p, x + 1] = value
            ysend[1 - p, 0, x : x + 1, :] = value[0:1, :]
            ysend[1 - p, 1, x : x + 1, :] = value[31:32, :]

    def step(t, c):
        p = lax.rem(t, 2)
        for copy in halo_x(p) + halo_y(p):
            copy.wait()
        for x in (0, 7):
            layer(t, p, x, False)
        for copy in halo_x(1 - p):
            copy.start()
        for x in range(1, 7):
            layer(t, p, x, False)
        for copy in halo_y(1 - p):
            copy.start()
        inject(t + 1)
        return c

    lax.fori_loop(0, 7, step, 0)
    for copy in halo_x(1) + halo_y(1):
        copy.wait()
    for x in range(8):
        layer(7, 1, x, True)

    pairs = []
    for a in range(4):
        both = (-2.0 / vel_ref[2 * a]) * acc[2 * a]
        pairs.append(both + (-2.0 / vel_ref[2 * a + 1]) * acc[2 * a + 1])
    high, low = halves(jnp.concatenate(pairs, axis=0))
    pool_y = (iota((128, 128), 0) == iota((128, 128), 1) // 2).astype(F32).astype(BF16)
    pool_z = (iota((128, 256), 0) == iota((128, 256), 1) // 2).astype(F32).astype(BF16)
    rows = jnp.dot(pool_y, high, preferred_element_type=F32) + jnp.dot(
        pool_y, low, preferred_element_type=F32
    )
    high, low = halves(rows)
    usend[...] = ((dot_nt(pool_z, high) + dot_nt(pool_z, low)) * 0.125).reshape(8, 16, 128)
    urecv[j] = usend[j]

    def spread(k):
        to = lax.rem(j + k, ny)
        return remote(usend.at[to], urecv.at[j], us.at[k], ur.at[k], (i, to))

    for k in range(1, ny):
        spread(k).start()
    for k in range(1, ny):
        spread(k).wait()
    strip = iota((16, 128), 1) // 16
    for a in range(4):
        total = jnp.zeros((16, 128), F32)
        for b in range(8):
            turn = (16 * b - 16 * a) % 128
            tile = urecv[b]
            moved = pltpu.roll(tile, turn, 1) if turn else tile
            total = jnp.where(strip == b, moved, total)
        sens_ref[a] = total


def shards(vel, dens, last, now, facc, res, owner, cell, offset):
    vm = pl.BlockSpec(memory_space=pltpu.VMEM)
    dma = pltpu.SemaphoreType.DMA
    sens, final = pl.pallas_call(
        kernel,
        name="adjoint",
        out_shape=(
            jax.ShapeDtypeStruct((4, 16, 128), F32),
            jax.ShapeDtypeStruct((8, 32, 256), F32),
        ),
        in_specs=[vm] * 4 + [pl.BlockSpec(memory_space=pl.ANY)] + [vm] * 4,
        out_specs=(vm, vm),
        scratch_shapes=[
            pltpu.VMEM((2, 10, 32, 256), F32),
            pltpu.VMEM((10, 32, 256), F32),
            pltpu.VMEM((2, 2, 8, 256), F32),
            pltpu.VMEM((2, 2, 8, 256), F32),
            pltpu.VMEM((2, 8, 256), F32),
            pltpu.VMEM((2, 8, 256), F32),
            pltpu.VMEM((7, 8, 32, 256), F32),
            pltpu.VMEM((8, 32, 256), F32),
            pltpu.VMEM((8, 32, 256), F32),
            pltpu.VMEM((8, 8, 32, 256), BF16),
            pltpu.VMEM((32, 8, 128), F32),
            pltpu.VMEM((32, 8, 128), F32),
            pltpu.VMEM((256, 512), F32),
            pltpu.VMEM((8, 1024), F32),
            pltpu.VMEM((256, 1024), BF16),
            pltpu.VMEM((256, 1024), BF16),
            pltpu.VMEM((8, 16, 128), F32),
            pltpu.VMEM((8, 16, 128), F32),
            dma((2, 4)), dma((2, 4)), dma((4,)), dma((4,)),
            dma((32,)), dma((32,)), dma((8,)), dma((8,)), dma(()),
        ],
        compiler_params=pltpu.CompilerParams(
            collective_id=0, has_side_effects=True, vmem_limit_bytes=48 << 20
        ),
    )(
        last, now, dens, vel, facc, res,
        owner.reshape(1, -1), cell.reshape(1, -1), offset.reshape(1, -1),
    )
    return sens, final


def solution(mesh):
    in_specs = (
        P("gx", "gy", None),
        P("gx", "gy", None),
        P("gx", "gy", None),
        P("gx", "gy", None),
        P(None, "gx", "gy", None),
        P(("gx", "gy"), None),
        P(("gx", "gy"), None),
        P(("gx", "gy")),
        P(("gx", "gy")),
    )
    out_specs = (P("gx", "gy", None), P("gx", "gy", None))
    return jax.shard_map(shards, mesh=mesh, in_specs=in_specs, out_specs=out_specs, check_vma=False)
```

```python
import functools

import jax
import jax.numpy as jnp
from jax import lax
from jax.experimental import pallas as pl
from jax.experimental.pallas import tpu as pltpu
from jax.sharding import PartitionSpec as P

MESH = pl.DeviceIdType.MESH
F32, BF16, I32 = jnp.float32, jnp.bfloat16, jnp.int32


def dot_nt(a, b):
    return lax.dot_general(a, b, (((1,), (1,)), ((), ())), preferred_element_type=F32)


def iota(shape, dim):
    return lax.broadcasted_iota(I32, shape, dim)


def halves(value):
    high = value.astype(BF16)
    return high, (value - high.astype(F32)).astype(BF16)


def build_messages(res_ref, owner, cell, offset, msg_ref, table_ref):
    row, k = iota((256, 128), 0), iota((256, 128), 1)
    gap = jnp.abs(k + row // 8 - 16 * (row % 8 + 1))
    weights = jnp.maximum(16 - gap, 0).astype(F32).astype(BF16)
    table_ref[...] = dot_nt(weights, res_ref[...])
    amp = jnp.zeros((8, 512), F32)
    for shift in range(32):
        amp = amp + jnp.where(offset == shift, table_ref[8 * shift : 8 * shift + 8, :], 0.0)
    amp = amp * (1.0 / 64.0)
    member = (iota((32, 512), 0) == owner).astype(F32)
    earlier = (iota((512, 512), 0) < iota((512, 512), 1)).astype(F32).astype(BF16)
    counts = jnp.dot(member.astype(BF16), earlier, preferred_element_type=F32)
    rank = jnp.sum(member * counts, axis=0, keepdims=True)
    slot = owner * 32 + rank.astype(I32)
    high, low = halves(amp)
    which = iota((16, 512), 0)
    digits = jnp.where(which == 0, cell // 256, jnp.where(which == 1, cell % 256, 0))
    payload = jnp.concatenate(
        [high.astype(F32), low.astype(F32), digits.astype(F32)], axis=0
    ).astype(BF16)
    place = (iota((1024, 512), 0) == slot).astype(F32).astype(BF16)
    packed = dot_nt(payload, place)
    lane = iota((8, 128), 1)
    for o in range(32):
        block = slice(128 * (o // 4), 128 * (o // 4) + 128)
        amps = packed[0:8, block] + packed[8:16, block]
        cells = packed[16:24, block]
        back = 32 * (o % 4)
        if back:
            amps = pltpu.roll(amps, 128 - back, 1)
        ahead = (32 - back) % 128
        if ahead:
            cells = pltpu.roll(cells, ahead, 1)
        msg_ref[o] = jnp.where(lane < 32, amps, cells)


def collect(recv_ref, amp_ref, xy_ref, z_ref):
    lane = iota((8, 128), 1)
    xs, zs = [], []
    for g in range(8):
        amps = jnp.zeros((8, 128), F32)
        cells = jnp.zeros((8, 128), F32)
        for q in range(4):
            tile = recv_ref[4 * g + q]
            here = (lane // 32) == q
            moved = pltpu.roll(tile, 32 * q, 1) if q else tile
            amps = jnp.where(here, moved, amps)
            turn = (32 * q - 32) % 128
            moved = pltpu.roll(tile, turn, 1) if turn else tile
            cells = jnp.where(here, moved, cells)
        amp_ref[:, 128 * g : 128 * g + 128] = amps
        xs.append(cells[0:1, :])
        zs.append(cells[1:2, :])
    rows = iota((256, 1024), 0).astype(F32)
    xy_ref[...] = (rows == jnp.concatenate(xs, axis=1)).astype(F32).astype(BF16)
    z_ref[...] = (rows == jnp.concatenate(zs, axis=1)).astype(F32).astype(BF16)


def couplings(density, speed, near):
    lane = iota(density.shape, density.ndim - 1)
    near = near + [
        (
            jnp.where(lane == 255, 0.0, pltpu.roll(density, 255, 1)),
            jnp.where(lane == 255, 0.0, 1.0),
        ),
        (jnp.where(lane == 0, 0.0, pltpu.roll(density, 1, 1)), jnp.where(lane == 0, 0.0, 1.0)),
    ]
    speed = 0.11 * speed
    stiff = speed * speed * density
    centre, weights = 2.0, []
    for value, inside in near:
        strength = stiff * (2.0 / (density + value))
        centre = centre - strength
        weights.append(strength * inside)
    return [centre] + weights


def advance(weight, w, xp, xm, yp, ym, prev, injected):
    value = weight(0) * w + (injected - prev)
    value = value + weight(1) * xp + weight(2) * xm
    value = value + weight(3) * yp + weight(4) * ym
    return value + weight(5) * pltpu.roll(w, 255, 1) + weight(6) * pltpu.roll(w, 1, 1)


def shifted(w, above, below):
    n = w.shape[0]
    row = iota(w.shape, 0)
    up = jnp.where(row == n - 1, above, pltpu.roll(w, n - 1, 0))
    down = jnp.where(row == 0, below, pltpu.roll(w, 1, 0))
    return up, down


def kernel(
    last_hbm, now_hbm, dens_hbm, vel_hbm, facc_hbm, res_hbm, owner_hbm, cell_hbm, offset_hbm,
    sens_ref, final_ref,
    vel, res_ref, owner_ref, cell_ref, offset_ref, rho, wave, acc, facc,
    coef, coefx, coefy, src_e, src_o,
    hx, hodd, yodd, ysend, yrecv, csend, crecv,
    sxr, sysend, syr, rhx, vhx, stsend, strecv, rcsend, rcrecv,
    msg, recv, table, amp, xy, zz, usend, urecv,
    xs, xr, es, er, gs, gr, cs, cr, as_, ar, us, ur, fs,
):
    i, j = lax.axis_index("gx"), lax.axis_index("gy")
    nx, ny = 32, 8
    xside = (lax.rem(i + nx - 1, nx), lax.rem(i + 1, nx))
    yside = (lax.rem(j + ny - 1, ny), lax.rem(j + 1, ny))
    barrier = pltpu.get_barrier_semaphore()

    loads = [
        pltpu.make_async_copy(src, dst, fs.at[n])
        for n, (src, dst) in enumerate(
            [
                (res_hbm, res_ref), (offset_hbm, offset_ref), (owner_hbm, owner_ref),
                (cell_hbm, cell_ref), (now_hbm, wave.at[0]), (dens_hbm, rho), (vel_hbm, vel),
                (last_hbm, wave.at[1]), (facc_hbm, facc),
            ]
        )
    ]
    for copy in loads:
        copy.start()

    def greet(device):
        pl.semaphore_signal(barrier, inc=1, device_id=device, device_id_type=MESH)

    def greet_x(k, c):
        greet((lax.rem(i + k, nx), j))
        return c

    def greet_y(k, c):
        greet((i, lax.rem(j + k, ny)))
        return c

    lax.fori_loop(1, nx, greet_x, 0)
    lax.fori_loop(1, ny, greet_y, 0)
    for a in range(2):
        for b in range(2):
            greet((xside[a], yside[b]))
    for copy in loads[:4]:
        copy.wait()
    build_messages(res_ref, owner_ref[...], cell_ref[...], offset_ref[...], msg, table)
    recv[i] = msg[i]
    for copy in loads[4:8]:
        copy.wait()

    def keep_rows(x, value):
        ysend[0, 0, x : x + 1, :] = value[0:1, :]
        ysend[0, 1, x : x + 1, :] = value[1:2, :]
        ysend[1, 0, x : x + 1, :] = value[31:32, :]
        ysend[1, 1, x : x + 1, :] = value[30:31, :]

    def keep_corners(dst, a, value):
        dst[2 * a] = value[0:1, :]
        dst[2 * a + 1] = value[31:32, :]

    for x in range(8):
        keep_rows(x, wave[0, x])
        for side, rows in enumerate(((0, 1), (31, 30))):
            near, far = rows
            stsend[side, 0, x : x + 1, :] = rho[x, near : near + 1, :]
            stsend[side, 1, x : x + 1, :] = rho[x, far : far + 1, :]
            stsend[side, 2, x : x + 1, :] = vel[x, near : near + 1, :]
            stsend[side, 3, x : x + 1, :] = wave[1, x, near : near + 1, :]
    for a in range(2):
        keep_corners(csend, a, wave[0, 7 * a])
        keep_corners(rcsend, a, rho[7 * a])
    pl.semaphore_wait(barrier, nx + ny + 2)

    def remote(src, dst, send, receive, device):
        return pltpu.make_async_remote_copy(
            src_ref=src, dst_ref=dst, send_sem=send, recv_sem=receive,
            device_id=device, device_id_type=MESH,
        )

    def scatter(k):
        to = lax.rem(i + k, nx)
        return remote(msg.at[to], recv.at[i], as_.at[k], ar.at[k], (to, j))

    def begin(k, c):
        scatter(k).start()
        return c

    def end(k, c):
        scatter(k).wait()
        return c

    lax.fori_loop(1, nx, begin, 0)

    def move_x(p):
        return [
            remote(wave.at[0, pl.ds(6 * a, 2)], hx.at[p, 1 - a], xs.at[p, a], xr.at[p, a],
                   (xside[a], j))
            for a in range(2)
        ]

    def move_y(p):
        return [
            remote(ysend.at[b], yrecv.at[p, 1 - b], xs.at[p, 2 + b], xr.at[p, 2 + b],
                   (i, yside[b]))
            for b in range(2)
        ]

    def move_c(p):
        return [
            remote(csend.at[2 * a + b], crecv.at[p, 3 - 2 * a - b], cs.at[p, 2 * a + b],
                   cr.at[p, 2 * a + b], (xside[a], yside[b]))
            for a in range(2) for b in range(2)
        ]

    def move_s(p):
        return [
            remote(src_e.at[7 * a], sxr.at[p, 1 - a], gs.at[p, a], gr.at[p, a], (xside[a], j))
            for a in range(2)
        ] + [
            remote(sysend.at[b], syr.at[p, 1 - b], gs.at[p, 2 + b], gr.at[p, 2 + b],
                   (i, yside[b]))
            for b in range(2)
        ]

    statics = []
    for a in range(2):
        statics += [
            (rho.at[pl.ds(6 * a, 2)], rhx.at[1 - a], (xside[a], j)),
            (vel.at[7 * a], vhx.at[1 - a], (xside[a], j)),
            (wave.at[1, 7 * a], hodd.at[1 - a], (xside[a], j)),
            (stsend.at[a], strecv.at[1 - a], (i, yside[a])),
        ]
        for b in range(2):
            n = 2 * a + b
            statics.append((rcsend.at[n], rcrecv.at[3 - n], (xside[a], yside[b])))
    statics = [
        remote(src, dst, es.at[n], er.at[n], to) for n, (src, dst, to) in enumerate(statics)
    ]
    for copy in statics + move_c(0) + move_x(0) + move_y(0):
        copy.start()
    acc[...] = jnp.zeros_like(acc)
    for copy in loads[8:] + statics:
        copy.wait()
    yodd[...] = strecv[:, 3]

    row = iota((32, 256), 0)
    row8 = iota((8, 256), 0)
    has_low, has_high = (j > 0).astype(F32), (j < ny - 1).astype(F32)
    has_left, has_right = (i > 0).astype(F32), (i < nx - 1).astype(F32)

    def along_y(density, above, below):
        up, down = shifted(density, above * has_high, below * has_low)
        return [
            (up, jnp.where(row == 31, has_high, 1.0)),
            (down, jnp.where(row == 0, has_low, 1.0)),
        ]

    def couple(x, xp, xm, first, final):
        density = rho[x]
        near = [(xp * final, final), (xm * first, first)]
        near += along_y(density, strecv[1, 0, pl.ds(x, 1), :], strecv[0, 0, pl.ds(x, 1), :])
        for n, value in enumerate(couplings(density, vel[x], near)):
            coef[n, x] = value

    def couple_inner(x, c):
        couple(x, rho[x + 1], rho[x - 1], 1.0, 1.0)
        return c

    couple(0, rho[1], rhx[0, 1], has_left, 1.0)
    couple(7, rhx[1, 0], rho[6], 1.0, has_right)
    lax.fori_loop(1, 7, couple_inner, 0)
    for a in range(2):
        density = rhx[a, 1 - a]
        outer, inner = rhx[a, a], rho[7 * a]
        xp, xm = (outer, inner) if a else (inner, outer)
        near = [(xp, 1.0), (xm, 1.0)] + along_y(density, rcrecv[2 * a + 1], rcrecv[2 * a])
        for n, value in enumerate(couplings(density, vhx[a], near)):
            coefx[a, n] = value
    for b in range(2):
        density = strecv[b, 0]
        outer, inner = strecv[b, 1], stsend[b, 0]
        yp, ym = (outer, inner) if b else (inner, outer)
        xp, xm = shifted(density, rcrecv[2 + b] * has_right, rcrecv[b] * has_left)
        near = [
            (xp, jnp.where(row8 == 7, has_right, 1.0)),
            (xm, jnp.where(row8 == 0, has_left, 1.0)),
            (yp, 1.0),
            (ym, 1.0),
        ]
        for n, value in enumerate(couplings(density, strecv[b, 2], near)):
            coefy[b, n] = value

    lax.fori_loop(1, nx, end, 0)
    collect(recv, amp, xy, zz)

    def inject(t, dst):
        high, low = halves(amp[pl.ds(t, 1), :])
        cells = xy[...]
        dst[...] = (dot_nt(cells * high, zz[...]) + dot_nt(cells * low, zz[...])).reshape(
            8, 32, 256
        )

    def prepare(t, p):
        inject(t, src_e)
        for x in range(8):
            sysend[0, x : x + 1, :] = src_e[x, 0:1, :]
            sysend[1, x : x + 1, :] = src_e[x, 31:32, :]
        for copy in move_s(p):
            copy.start()
        inject(t + 1, src_o)

    prepare(0, 0)

    def even_layer(t, p, x):
        w = wave[0, x]
        yp, ym = shifted(w, yrecv[p, 1, 0, x : x + 1, :], yrecv[p, 0, 0, x : x + 1, :])
        xp = wave[0, x + 1] if x < 7 else hx[p, 1, 0]
        xm = wave[0, x - 1] if x > 0 else hx[p, 0, 1]
        value = advance(lambda n: coef[n, x], w, xp, xm, yp, ym, wave[1, x], src_e[x])
        acc[x] += value * facc[t, x].astype(F32)
        wave[1, x] = value

    def odd_layer(t, x, out):
        w = wave[1, x]
        yp, ym = shifted(w, yodd[1, x : x + 1, :], yodd[0, x : x + 1, :])
        xp = wave[1, x + 1] if x < 7 else hodd[1]
        xm = wave[1, x - 1] if x > 0 else hodd[0]
        value = advance(lambda n: coef[n, x], w, xp, xm, yp, ym, wave[0, x], src_o[x])
        acc[x] += value * facc[t, x].astype(F32)
        if out:
            final_ref[x] = value
        else:
            wave[0, x] = value
            keep_rows(x, value)
            if x in (0, 7):
                keep_corners(csend, x // 7, value)

    def halo_layers(p):
        for a in range(2):
            w = hx[p, a, 1 - a]
            outer, inner = hx[p, a, a], wave[0, 7 * a]
            xp, xm = (outer, inner) if a else (inner, outer)
            yp, ym = shifted(w, crecv[p, 2 * a + 1], crecv[p, 2 * a])
            hodd[a] = advance(lambda n: coefx[a, n], w, xp, xm, yp, ym, hodd[a], sxr[p, a])
        for b in range(2):
            w = yrecv[p, b, 0]
            outer, inner = yrecv[p, b, 1], ysend[b, 0]
            yp, ym = (outer, inner) if b else (inner, outer)
            xp, xm = shifted(w, crecv[p, 2 + b], crecv[p, b])
            yodd[b] = advance(lambda n: coefy[b, n], w, xp, xm, yp, ym, yodd[b], syr[p, b])

    def pair(r, p, final):
        for copy in move_x(p) + move_y(p):
            copy.wait()
        for x in range(8):
            even_layer(2 * r, p, x)
        for copy in move_c(p) + move_s(p):
            copy.wait()
        halo_layers(p)
        if final:
            for x in range(8):
                odd_layer(2 * r + 1, x, True)
            return
        for x in (0, 7, 1, 6):
            odd_layer(2 * r + 1, x, False)
        for copy in move_c(1 - p) + move_x(1 - p):
            copy.start()
        for x in range(2, 6):
            odd_layer(2 * r + 1, x, False)
        for copy in move_y(1 - p):
            copy.start()
        prepare(2 * r + 2, 1 - p)

    def pair_step(r, c):
        pair(r, lax.rem(r, 2), False)
        return c

    lax.fori_loop(0, 3, pair_step, 0)
    pair(3, 1, True)

    pairs = []
    for a in range(4):
        both = (-2.0 / vel[2 * a]) * acc[2 * a]
        pairs.append(both + (-2.0 / vel[2 * a + 1]) * acc[2 * a + 1])
    high, low = halves(jnp.concatenate(pairs, axis=0))
    pool_y = (iota((128, 128), 0) == iota((128, 128), 1) // 2).astype(F32).astype(BF16)
    pool_z = (iota((128, 256), 0) == iota((128, 256), 1) // 2).astype(F32).astype(BF16)
    rows = jnp.dot(pool_y, high, preferred_element_type=F32) + jnp.dot(
        pool_y, low, preferred_element_type=F32
    )
    high, low = halves(rows)
    usend[...] = ((dot_nt(pool_z, high) + dot_nt(pool_z, low)) * 0.125).reshape(8, 16, 128)
    urecv[j] = usend[j]

    def spread(k):
        to = lax.rem(j + k, ny)
        return remote(usend.at[to], urecv.at[j], us.at[k], ur.at[k], (i, to))

    for k in range(1, ny):
        spread(k).start()
    for k in range(1, ny):
        spread(k).wait()
    strip = iota((16, 128), 1) // 16
    for a in range(4):
        total = jnp.zeros((16, 128), F32)
        for b in range(8):
            turn = (16 * b - 16 * a) % 128
            tile = urecv[b]
            moved = pltpu.roll(tile, turn, 1) if turn else tile
            total = jnp.where(strip == b, moved, total)
        sens_ref[a] = total


def shards(vel, dens, last, now, facc, res, owner, cell, offset):
    vm = pl.BlockSpec(memory_space=pltpu.VMEM)
    dma = pltpu.SemaphoreType.DMA
    field, plane, line = (8, 32, 256), (32, 256), (8, 256)
    f32 = lambda *shape: pltpu.VMEM(shape, F32)
    sens, final = pl.pallas_call(
        kernel,
        name="adjoint",
        out_shape=(
            jax.ShapeDtypeStruct((4, 16, 128), F32),
            jax.ShapeDtypeStruct(field, F32),
        ),
        in_specs=[pl.BlockSpec(memory_space=pltpu.HBM)] * 9,
        out_specs=(vm, vm),
        scratch_shapes=[
            f32(*field), pltpu.VMEM((512, 128), BF16), pltpu.VMEM((1, 512), I32),
            pltpu.VMEM((1, 512), I32), pltpu.VMEM((1, 512), I32),
            f32(*field), f32(2, *field), f32(*field), pltpu.VMEM((8, *field), BF16),
            f32(7, *field), f32(2, 7, *plane), f32(2, 7, *line), f32(*field), f32(*field),
            f32(2, 2, 2, *plane), f32(2, *plane), f32(2, *line), f32(2, 2, *line),
            f32(2, 2, 2, *line), f32(4, 1, 256), f32(2, 4, 1, 256),
            f32(2, 2, *plane), f32(2, *line), f32(2, 2, *line),
            f32(2, 2, *plane), f32(2, *plane), f32(2, 4, *line), f32(2, 4, *line),
            f32(4, 1, 256), f32(4, 1, 256),
            f32(32, 8, 128), f32(32, 8, 128), f32(256, 512), f32(8, 1024),
            pltpu.VMEM((256, 1024), BF16), pltpu.VMEM((256, 1024), BF16),
            f32(8, 16, 128), f32(8, 16, 128),
            dma((2, 4)), dma((2, 4)), dma((12,)), dma((12,)), dma((2, 4)), dma((2, 4)),
            dma((2, 4)), dma((2, 4)), dma((32,)), dma((32,)), dma((8,)), dma((8,)), dma((9,)),
        ],
        compiler_params=pltpu.CompilerParams(
            collective_id=0, has_side_effects=True, vmem_limit_bytes=67043328
        ),
    )(
        last, now, dens, vel, facc, res,
        owner.reshape(1, -1), cell.reshape(1, -1), offset.reshape(1, -1),
    )
    return sens, final


def solution(mesh):
    in_specs = (
        P("gx", "gy", None),
        P("gx", "gy", None),
        P("gx", "gy", None),
        P("gx", "gy", None),
        P(None, "gx", "gy", None),
        P(("gx", "gy"), None),
        P(("gx", "gy"), None),
        P(("gx", "gy")),
        P(("gx", "gy")),
    )
    out_specs = (P("gx", "gy", None), P("gx", "gy", None))
    return jax.shard_map(shards, mesh=mesh, in_specs=in_specs, out_specs=out_specs, check_vma=False)
```
